512 devices in a mesh: tm: 32 (over y, z_lo), lon: 16 (over x, z_hi, core).
Axes of the slice: x: 4, y: 4, z: 16 (z_hi: 2, z_lo: 8; z = z_hi * 8 + z_lo), core: 2. Of those that a mesh axis runs over, the one named last changes fastest.
Arguments:
- field: bfloat16 [4096, 288, 512], P('tm', 'lon'), may hold values from -15 to 15
- omega: bfloat16 [288, 512, 64], P('lon'), may hold values from -0.015625 to 0.015625
Outputs:
- projected: bfloat16 [4096, 288, 512], P('tm', 'lon')
- series: float32 [4096, 64], P('tm')
The draws below stay inside these ranges and needn't reach their ends.
All inputs are finite; a program needn't handle non-finite values.
Results may differ from the reference program's by a relative error of at most 0.0082.
Values may be sent and summed in bfloat16 or wider, within the bound.
A program may use at most 64 MiB of HBM per device.

```python
import math
import jax
import jax.numpy as jnp
from jax import lax

NLAT = 32
NVAR = 16
HALF = 15
RANK = 64
DAYS = 4096
NLON = 288
COLS = 512


def block_scale(key, dims, cuts, least, high):
    def one(position, parts):
        draws = jax.random.uniform(jax.random.fold_in(jax.random.fold_in(key, 6), position), (parts,), jnp.float32, least / len(cuts), high / len(cuts))
        return jnp.repeat(jnp.exp(draws), dims[position] // parts).reshape((-1,) + (1,) * (len(dims) - position - 1))

    factor_of = one(*cuts[0])
    for cut in cuts[1:]:
        factor_of = factor_of * one(*cut)
    return factor_of


def noise(stream_key, dims, deviation, reach, cuts=(), held_as=jnp.bfloat16):
    factor_of = block_scale(stream_key, dims, cuts, -0.22, 0.18) if cuts else 1.0
    drawn = jax.random.normal(stream_key, dims, jnp.float32) * deviation * factor_of
    return jnp.minimum(jnp.maximum(drawn, -reach), reach).astype(held_as)


def setup_inputs(seed: int = 0) -> dict:
    arg_keys = jax.random.split(jax.random.key(seed), 3)
    return {
        "field": noise(arg_keys[0], (DAYS, NLON, COLS), 3.0, 15.0, ((0, 32), (1, 16))),
        "omega": noise(arg_keys[1], (NLON, COLS, RANK), (NLON * COLS) ** -0.5, 0.015625, ((0, 16),)),
    }


def band_taps(half):
    offsets = jnp.arange(-half, half + 1).astype(jnp.float32)
    safe = jnp.where(offsets == 0, 1.0, offsets)
    core = (jnp.sin(2.0 * math.pi * safe / 3.0) - jnp.sin(2.0 * math.pi * safe / 30.0)) / (math.pi * safe)
    core = jnp.where(offsets == 0, 2.0 * (1.0 / 3.0 - 1.0 / 30.0), core)
    spread = math.pi * safe / (half + 1)
    sigma = jnp.where(offsets == 0, 1.0, jnp.sin(spread) / spread)
    return (core * sigma).astype(jnp.bfloat16)

def reference(field, omega):
    taps = band_taps(HALF).astype(jnp.float32)
    pieces = []
    sketch = jnp.zeros((DAYS, RANK), jnp.float32)
    for level in range(NVAR):
        block = field[:, :, level * NLAT:(level + 1) * NLAT].astype(jnp.float32)
        padded = jnp.pad(block, ((HALF, HALF), (0, 0), (0, 0)))
        filtered = jnp.zeros((DAYS, NLON, NLAT), jnp.float32)
        for offset in range(2 * HALF + 1):
            filtered = filtered + taps[offset] * padded[offset:offset + DAYS]
        across = jnp.roll(filtered, 1, 1) + 2.0 * filtered + jnp.roll(filtered, -1, 1)
        lat_pad = jnp.pad(across, ((0, 0), (0, 0), (1, 1)))
        smooth = (lat_pad[:, :, :-2] + 2.0 * lat_pad[:, :, 1:-1] + lat_pad[:, :, 2:]) * 0.0625
        anomalies = smooth.astype(jnp.bfloat16).reshape(DAYS, NLON * NLAT)
        weights = omega[:, level * NLAT:(level + 1) * NLAT, :].reshape(NLON * NLAT, RANK)
        sketch = sketch + jnp.dot(anomalies.astype(jnp.float32), weights.astype(jnp.float32), preferred_element_type=jnp.float32)
        pieces.append(anomalies)
    gram = jnp.dot(sketch.T, sketch, precision=lax.Precision.HIGHEST)
    lower = jnp.linalg.cholesky(gram)
    basis = jax.scipy.linalg.solve_triangular(lower, sketch.T, lower=True).T
    series = basis * math.sqrt(DAYS)
    basis_b = basis.astype(jnp.bfloat16)
    outputs = []
    for level in range(NVAR):
        patterns = jnp.dot(pieces[level].T.astype(jnp.float32), basis_b.astype(jnp.float32), preferred_element_type=jnp.float32).astype(jnp.bfloat16)
        recon = jnp.dot(basis_b.astype(jnp.float32), patterns.T.astype(jnp.float32), preferred_element_type=jnp.float32).astype(jnp.bfloat16)
        outputs.append(recon.reshape(DAYS, NLON, NLAT))
    projected = jnp.concatenate(outputs, axis=2)
    return (projected, series)
```

```python
import math

import jax
import jax.numpy as jnp
import ml_dtypes
import numpy as np
from jax import lax
from jax.experimental import pallas as pl
from jax.experimental.pallas import tpu as pltpu
from jax.sharding import PartitionSpec as P

NLAT = 32
HALF = 15
RANK = 64
NY, NZ, NX = 4, 8, 4
HI = lax.Precision.HIGHEST
MESH = pl.DeviceIdType.MESH


def toeplitz_blocks():
    offsets = np.arange(-HALF, HALF + 1).astype(np.float64)
    safe = np.where(offsets == 0, 1.0, offsets)
    core = (np.sin(2.0 * math.pi * safe / 3.0) - np.sin(2.0 * math.pi * safe / 30.0)) / (math.pi * safe)
    core = np.where(offsets == 0, 2.0 * (1.0 / 3.0 - 1.0 / 30.0), core)
    spread = math.pi * safe / (HALF + 1)
    sigma = np.where(offsets == 0, 1.0, np.sin(spread) / spread)
    taps = (core * sigma).astype(np.float32).astype(ml_dtypes.bfloat16).astype(np.float32)
    rows = np.arange(384)[:, None] - 128
    cols = np.arange(128)[None, :]
    diff = rows - cols
    inside = np.abs(diff) <= HALF
    return np.where(inside, taps[np.clip(diff + HALF, 0, 2 * HALF)], 0.0).astype(np.float32)


def halves(value):
    high = value.astype(jnp.bfloat16)
    low = (value - high.astype(jnp.float32)).astype(jnp.bfloat16)
    return jnp.concatenate([high, low], axis=0)


def contract_last(a, b, precision=None):
    return lax.dot_general(a, b, (((1,), (1,)), ((), ())), precision=precision, preferred_element_type=jnp.float32)


def contract_first(a, b, precision=None):
    return lax.dot_general(a, b, (((0,), (0,)), ((), ())), precision=precision, preferred_element_type=jnp.float32)


def matmul(a, b, precision=None):
    return jnp.dot(a, b, precision=precision, preferred_element_type=jnp.float32)


def lat_smooth(tile):
    lane = lax.broadcasted_iota(jnp.int32, tile.shape, tile.ndim - 1) % NLAT
    left = jnp.where(lane == 0, 0.0, pltpu.roll(tile, 1, tile.ndim - 1))
    right = jnp.where(lane == NLAT - 1, 0.0, pltpu.roll(tile, 127, tile.ndim - 1))
    return left + 2.0 * tile + right


def kernel(
    field, omega, toeplitz, patterns_out, basis_out, series_out,
    fhalo, osm, va, cbuf, xbuf, zq, edges, edge_in, gbuf, gin, ysend, yrecv, zsend, zrecv, gathered, elim,
    halo_s, halo_r, core_s, core_r, x_s, x_r, zq_s, zq_r, edge_s, edge_r, g_s, g_r, y_s, y_r, z_s, z_r,
    az_s, az_r, ay_s, ay_r,
):
    bands = field.shape[0]
    tm = lax.axis_index("tm")
    lon = lax.axis_index("lon")
    days_blocks = NY * NZ
    y, z = tm // NZ, tm % NZ
    nlon = 16
    next_lon, prev_lon = (lon + 1) % nlon, (lon + nlon - 1) % nlon
    core_lon = lon + 1 - 2 * (lon % 2)
    zh_lon = lon + 2 - 4 * ((lon // 2) % 2)
    x = lon // 4
    x_lons = [((x + d) % NX) * 4 + lon % 4 for d in range(1, NX)]
    next_tm, prev_tm = (tm + 1) % days_blocks, (tm + days_blocks - 1) % days_blocks
    y_tms = [((y + d) % NY) * NZ + z for d in range(1, NY)]
    z_tms = [y * NZ + (z + d) % NZ for d in range(1, NZ)]

    def remote(src, dst, send, recv, to_tm, to_lon):
        copy = pltpu.make_async_remote_copy(
            src_ref=src, dst_ref=dst, send_sem=send, recv_sem=recv,
            device_id=(to_tm, to_lon), device_id_type=MESH,
        )
        copy.start()
        return copy

    barrier = pltpu.get_barrier_semaphore()
    partners = [(tm, next_lon), (tm, prev_lon), (tm, zh_lon)]
    partners += [(tm, other) for other in x_lons]
    partners += [(t, l) for t in (next_tm, prev_tm) for l in (lon, zh_lon)]
    partners += [(t, lon) for t in y_tms + z_tms]
    for partner in partners:
        pl.semaphore_signal(barrier, inc=1, device_id=partner, device_id_type=MESH)

    osm[0] = jnp.zeros_like(osm[0])
    osm[bands + 1] = jnp.zeros_like(osm[0])

    def smooth_omega(l, carry):
        for c in range(4):
            tile = omega[l, :, c * 128:(c + 1) * 128].astype(jnp.float32)
            osm[l + 1, :, c * 128:(c + 1) * 128] = lat_smooth(tile) * 0.0625
        return carry

    lax.fori_loop(0, bands, smooth_omega, 0)
    pl.semaphore_wait(barrier, len(partners))

    up = remote(field.at[bands - 1], fhalo.at[0], halo_s.at[0], halo_r.at[0], tm, next_lon)
    down = remote(field.at[0], fhalo.at[1], halo_s.at[1], halo_r.at[1], tm, prev_lon)

    def sketch_term(l, acc):
        weights = osm[l] + 2.0 * osm[l + 1] + osm[l + 2]
        return acc + contract_last(halves(weights), field[l])

    acc = lax.fori_loop(0, bands, sketch_term, jnp.zeros((2 * RANK, 128), jnp.float32))
    up.wait()
    acc = acc + contract_last(halves(osm[1]), fhalo[0])
    down.wait()
    acc = acc + contract_last(halves(osm[bands]), fhalo[1])

    cbuf[0] = acc[:RANK] + acc[RANK:]
    copy = remote(cbuf.at[0], cbuf.at[1], core_s, core_r, tm, core_lon)
    copy.wait()
    xbuf[x] = cbuf[0] + cbuf[1]
    copies = [
        remote(xbuf.at[x], xbuf.at[x], x_s.at[i], x_r.at[i], tm, other) for i, other in enumerate(x_lons)
    ]
    for copy in copies:
        copy.wait()
    total = (xbuf[0] + xbuf[1]) + (xbuf[2] + xbuf[3])
    zq[0] = total
    full = remote(zq.at[0], zq.at[1], zq_s, zq_r, tm, zh_lon)
    lane16 = lax.broadcasted_iota(jnp.int32, (16, 128), 1)
    first = jnp.zeros((16, 128), jnp.float32)
    last = jnp.zeros((16, 128), jnp.float32)
    for g in range(4):
        piece = total[16 * g:16 * (g + 1)]
        mine = lane16 // 32 == g
        first = jnp.where(mine, piece if g == 0 else pltpu.roll(piece, 32 * g, 1), first)
        last = jnp.where(mine, piece if g == 3 else pltpu.roll(piece, 32 * (g + 1), 1), last)
    edges[0] = last
    edges[1] = first
    copies = []
    for side, to_tm in ((0, next_tm), (1, prev_tm)):
        for part, to_lon in ((0, lon), (1, zh_lon)):
            i = 2 * side + part
            copies.append(remote(edges.at[side], edge_in.at[i], edge_s.at[i], edge_r.at[i], to_tm, to_lon))
    full.wait()
    for copy in copies:
        copy.wait()
    before = edge_in[0] + edge_in[1]
    after = edge_in[2] + edge_in[3]
    low, high = [], []
    for g in range(4):
        low.append(jnp.where(lane16 >= 96, before if g == 3 else pltpu.roll(before, 96 - 32 * g, 1), 0.0))
        high.append(jnp.where(lane16 < 32, after if g == 0 else pltpu.roll(after, 128 - 32 * g, 1), 0.0))
    has_low = (tm > 0).astype(jnp.float32)
    has_high = (tm < days_blocks - 1).astype(jnp.float32)
    low = jnp.concatenate(low, axis=0) * has_low
    high = jnp.concatenate(high, axis=0) * has_high
    raw = zq[0] + zq[1]

    t_low, t_mid, t_high = (toeplitz[128 * i:128 * (i + 1)] for i in range(3))
    sketch = matmul(low, t_low, HI) + matmul(raw, t_mid, HI) + matmul(high, t_high, HI)
    sketch_low = (matmul(low, t_mid, HI) + matmul(raw, t_high, HI)) * has_low
    sketch_high = (matmul(raw, t_low, HI) + matmul(high, t_mid, HI)) * has_high
    back = matmul(sketch_low, t_low, HI) + matmul(sketch, t_mid, HI) + matmul(sketch_high, t_high, HI)
    gram = contract_last(sketch, sketch, HI)
    gbuf[0] = jnp.concatenate([gram, jnp.zeros((RANK, 64), jnp.float32)], axis=1)

    back2 = halves(back)

    def term(block):
        both = matmul(back2, block)
        return both[:RANK] + both[RANK:]

    va[0] = term(fhalo[0])
    va[bands + 1] = term(fhalo[1])

    def pattern_term(l, carry):
        va[l + 1] = term(field[l])
        return carry

    lax.fori_loop(0, bands, pattern_term, 0)

    def pack(pair, carry):
        l = 2 * pair
        one, two, three, four = va[l], va[l + 1], va[l + 2], va[l + 3]
        even = one + 2.0 * two + three
        odd = two + 2.0 * three + four
        for c in range(NY):
            for k in range(NZ):
                rows, cols = slice(8 * k, 8 * k + 8), slice(128 * c, 128 * c + 128)
                ysend[c, k, pair] = jnp.concatenate([even[rows, cols], odd[rows, cols]], axis=0).astype(jnp.bfloat16)
        return carry

    lax.fori_loop(0, bands // 2, pack, 0)

    y_copies = []
    for d in range(1, NY):
        y_copies.append(
            remote(ysend.at[(y + d) % NY], yrecv.at[d - 1], y_s.at[d - 1], y_r.at[d - 1], y_tms[d - 1], lon)
        )

    steps = [(1, z, 1), (2, z, 2), (4, z, 4), (1, y, NZ), (2, y, 2 * NZ)]
    for i, (bit, coord, stride) in enumerate(steps):
        to_tm = tm + stride - 2 * stride * ((coord // bit) % 2)
        copy = remote(gbuf.at[i], gin.at[i], g_s.at[i], g_r.at[i], to_tm, lon)
        copy.wait()
        gbuf[i + 1] = gbuf[i] + gin[i]

    for copy in y_copies:
        copy.wait()

    def sum_y(k, carry):
        value = ysend[y, k].astype(jnp.float32)
        for d in range(NY - 1):
            value = value + yrecv[d, k].astype(jnp.float32)
        zsend[k] = value.astype(jnp.bfloat16)
        return carry

    lax.fori_loop(0, NZ, sum_y, 0)
    z_copies = []
    for d in range(1, NZ):
        z_copies.append(
            remote(zsend.at[(z + d) % NZ], zrecv.at[d - 1], z_s.at[d - 1], z_r.at[d - 1], z_tms[d - 1], lon)
        )

    lane = lax.broadcasted_iota(jnp.int32, (RANK, 128), 1)
    row_of = lax.broadcasted_iota(jnp.int32, (RANK, 128), 0)
    elim[...] = jnp.where(lane == row_of + RANK, 1.0, gbuf[len(steps)])

    def eliminate(j, carry):
        matrix = elim[...]
        row = elim[pl.ds(j, 1), :]
        column = jnp.sum(jnp.where(lane == j, matrix, 0.0), axis=1, keepdims=True)
        pivot = jnp.sum(jnp.where(lane[:1] == j, row, 0.0), axis=1, keepdims=True)
        factor = jnp.where(row_of[:, :1] > j, column / pivot, 0.0)
        elim[...] = matrix - factor * row
        return carry

    lax.fori_loop(0, RANK, eliminate, 0)
    matrix = elim[...]
    diagonal = jnp.sum(jnp.where(lane == row_of, matrix, 0.0), axis=1, keepdims=True)
    inverse = (matrix / jnp.sqrt(diagonal))[:, RANK:]
    basis = matmul(inverse, sketch, HI)
    series_out[...] = basis * math.sqrt(128 * days_blocks)
    basis_out[...] = contract_first(inverse, basis, HI).astype(jnp.bfloat16)

    for copy in z_copies:
        copy.wait()
    value = zsend[z].astype(jnp.float32)
    for d in range(NZ - 1):
        value = value + zrecv[d].astype(jnp.float32)
    value = lat_smooth(value.reshape(bands // 2 * 16, 128)) * 0.0625
    gathered[y, z] = value.reshape(bands // 2, 16, 128).astype(jnp.bfloat16)

    az = [
        remote(gathered.at[y, z], gathered.at[y, z], az_s.at[i], az_r.at[i], other, lon)
        for i, other in enumerate(z_tms)
    ]
    ay = []

    def over_y(i, k):
        for d in range(1, NY):
            ay.append(
                remote(gathered.at[y, k], gathered.at[y, k], ay_s.at[i, d - 1], ay_r.at[i, d - 1], y_tms[d - 1], lon)
            )

    over_y(0, z)
    for d in (1, 7, 2, 6, 3, 5, 4):
        az[d - 1].wait_recv()
        over_y(d, (z + NZ - d) % NZ)
    for copy in az:
        copy.wait_send()
    for copy in ay:
        copy.wait()

    def unpack(pair, carry):
        for c in range(NY):
            both = [gathered[c, k, pair].astype(jnp.float32) for k in range(NZ)]
            cols = slice(128 * c, 128 * c + 128)
            for i in range(2):
                rows = jnp.concatenate([block[8 * i:8 * i + 8] for block in both], axis=0)
                patterns_out[2 * pair + i, :, cols] = rows.astype(jnp.bfloat16)
        return carry

    lax.fori_loop(0, bands // 2, unpack, 0)


def project(basis, patterns, out):
    for i in range(patterns.shape[0]):
        out[i] = contract_first(basis[...], patterns[i]).astype(jnp.bfloat16)


def local(field, omega):
    days, bands, cols = field.shape
    pairs = bands // 2
    f32, bf16 = jnp.float32, jnp.bfloat16
    dma = pltpu.SemaphoreType.DMA
    chunk = (pairs, 16, 128)
    vmem = pl.BlockSpec(memory_space=pltpu.VMEM)
    patterns, basis, series = pl.pallas_call(
        kernel,
        out_shape=(
            jax.ShapeDtypeStruct((bands, RANK, cols), bf16),
            jax.ShapeDtypeStruct((RANK, days), bf16),
            jax.ShapeDtypeStruct((RANK, days), f32),
        ),
        in_specs=[vmem] * 3,
        out_specs=(vmem,) * 3,
        scratch_shapes=[
            pltpu.VMEM((2, days, cols), bf16),
            pltpu.VMEM((bands + 2, RANK, cols), f32),
            pltpu.VMEM((bands + 2, RANK, cols), f32),
            pltpu.VMEM((2, RANK, days), f32),
            pltpu.VMEM((NX, RANK, days), f32),
            pltpu.VMEM((2, RANK, days), f32),
            pltpu.VMEM((2, 16, days), f32),
            pltpu.VMEM((4, 16, days), f32),
            pltpu.VMEM((6, RANK, 128), f32),
            pltpu.VMEM((5, RANK, 128), f32),
            pltpu.VMEM((NY, NZ) + chunk, bf16),
            pltpu.VMEM((NY - 1, NZ) + chunk, bf16),
            pltpu.VMEM((NZ,) + chunk, bf16),
            pltpu.VMEM((NZ - 1,) + chunk, bf16),
            pltpu.VMEM((NY, NZ) + chunk, bf16),
            pltpu.VMEM((RANK, 128), f32),
            dma((2,)), dma((2,)), dma, dma, dma((3,)), dma((3,)), dma, dma, dma((4,)), dma((4,)),
            dma((5,)), dma((5,)), dma((3,)), dma((3,)), dma((7,)), dma((7,)), dma((7,)), dma((7,)),
            dma((8, 3)), dma((8, 3)),
        ],
        compiler_params=pltpu.CompilerParams(collective_id=0, has_side_effects=True),
        name="subspace",
    )(jnp.transpose(field, (1, 0, 2)), jnp.transpose(omega, (0, 2, 1)), jnp.asarray(toeplitz_blocks()))
    step = 3
    projected = pl.pallas_call(
        project,
        grid=(bands // step,),
        out_shape=jax.ShapeDtypeStruct((bands, days, cols), bf16),
        in_specs=[
            pl.BlockSpec((RANK, days), lambda i: (0, 0)),
            pl.BlockSpec((step, RANK, cols), lambda i: (i, 0, 0)),
        ],
        out_specs=pl.BlockSpec((step, days, cols), lambda i: (i, 0, 0)),
        name="project",
    )(basis, patterns)
    return jnp.transpose(projected, (1, 0, 2)), series.T


def solution(mesh):
    in_specs = (P("tm", "lon", None), P("lon", None, None))
    out_specs = (P("tm", "lon", None), P("tm", None))
    return jax.shard_map(local, mesh=mesh, in_specs=in_specs, out_specs=out_specs, check_vma=False)
```

```python
import math

import jax
import jax.numpy as jnp
import ml_dtypes
import numpy as np
from jax import lax
from jax.experimental import pallas as pl
from jax.experimental.pallas import tpu as pltpu
from jax.sharding import PartitionSpec as P

NLAT = 32
HALF = 15
RANK = 64
NY, NZ, NX = 4, 8, 4
HI = lax.Precision.HIGHEST
MESH = pl.DeviceIdType.MESH


def toeplitz_blocks():
    offsets = np.arange(-HALF, HALF + 1).astype(np.float64)
    safe = np.where(offsets == 0, 1.0, offsets)
    core = (np.sin(2.0 * math.pi * safe / 3.0) - np.sin(2.0 * math.pi * safe / 30.0)) / (math.pi * safe)
    core = np.where(offsets == 0, 2.0 * (1.0 / 3.0 - 1.0 / 30.0), core)
    spread = math.pi * safe / (HALF + 1)
    sigma = np.where(offsets == 0, 1.0, np.sin(spread) / spread)
    taps = (core * sigma).astype(np.float32).astype(ml_dtypes.bfloat16).astype(np.float32)
    rows = np.arange(384)[:, None] - 128
    cols = np.arange(128)[None, :]
    diff = rows - cols
    inside = np.abs(diff) <= HALF
    return np.where(inside, taps[np.clip(diff + HALF, 0, 2 * HALF)], 0.0).astype(np.float32)


def halves(value):
    high = value.astype(jnp.bfloat16)
    low = (value - high.astype(jnp.float32)).astype(jnp.bfloat16)
    return jnp.concatenate([high, low], axis=0)


def contract_last(a, b, precision=None):
    return lax.dot_general(a, b, (((1,), (1,)), ((), ())), precision=precision, preferred_element_type=jnp.float32)


def contract_first(a, b, precision=None):
    return lax.dot_general(a, b, (((0,), (0,)), ((), ())), precision=precision, preferred_element_type=jnp.float32)


def matmul(a, b, precision=None):
    return jnp.dot(a, b, precision=precision, preferred_element_type=jnp.float32)


def lat_smooth(tile):
    lane = lax.broadcasted_iota(jnp.int32, tile.shape, tile.ndim - 1) % NLAT
    left = jnp.where(lane == 0, 0.0, pltpu.roll(tile, 1, tile.ndim - 1))
    right = jnp.where(lane == NLAT - 1, 0.0, pltpu.roll(tile, 127, tile.ndim - 1))
    return left + 2.0 * tile + right


def kernel(
    field, omega, toeplitz, patterns_out, basis_out, series_out,
    ohalo, osm, fy, ubuf, cbuf, xbuf, zq, edges, edge_in, gbuf, gin, zsend, zrecv, lon_edge, lon_in, gathered, rims, elim,
    halo_s, halo_r, core_s, core_r, x_s, x_r, zq_s, zq_r, edge_s, edge_r, g_s, g_r, f_s, f_r, u_s, u_r, z_s, z_r,
    le_s, le_r, az_s, az_r, ay_s, ay_r, rz_s, rz_r, ry_s, ry_r,
):
    bands = field.shape[0]
    tm = lax.axis_index("tm")
    lon = lax.axis_index("lon")
    days_blocks = NY * NZ
    y, z = tm // NZ, tm % NZ
    nlon = 16
    next_lon, prev_lon = (lon + 1) % nlon, (lon + nlon - 1) % nlon
    core_lon = lon + 1 - 2 * (lon % 2)
    zh_lon = lon + 2 - 4 * ((lon // 2) % 2)
    x = lon // 4
    x_lons = [((x + d) % NX) * 4 + lon % 4 for d in range(1, NX)]
    next_tm, prev_tm = (tm + 1) % days_blocks, (tm + days_blocks - 1) % days_blocks
    y_tms = [((y + d) % NY) * NZ + z for d in range(1, NY)]
    z_tms = [y * NZ + (z + d) % NZ for d in range(1, NZ)]

    def remote(src, dst, send, recv, to_tm, to_lon):
        copy = pltpu.make_async_remote_copy(
            src_ref=src, dst_ref=dst, send_sem=send, recv_sem=recv,
            device_id=(to_tm, to_lon), device_id_type=MESH,
        )
        copy.start()
        return copy

    barrier = pltpu.get_barrier_semaphore()
    partners = [(tm, next_lon), (tm, prev_lon), (tm, zh_lon)]
    partners += [(tm, other) for other in x_lons]
    partners += [(t, l) for t in (next_tm, prev_tm) for l in (lon, zh_lon)]
    partners += [(t, lon) for t in y_tms + z_tms]
    for partner in partners:
        pl.semaphore_signal(barrier, inc=1, device_id=partner, device_id_type=MESH)

    osm[0] = jnp.zeros_like(osm[0])
    osm[bands + 1] = jnp.zeros_like(osm[0])

    def smooth_omega(l, carry):
        for c in range(4):
            tile = omega[l, :, c * 128:(c + 1) * 128].astype(jnp.float32)
            osm[l + 1, :, c * 128:(c + 1) * 128] = lat_smooth(tile) * 0.0625
        return carry

    lax.fori_loop(0, bands, smooth_omega, 0)

    def sketch_term(l, acc):
        weights = osm[l] + 2.0 * osm[l + 1] + osm[l + 2]
        return acc + contract_last(halves(weights), field[l])

    acc = lax.fori_loop(0, bands, sketch_term, jnp.zeros((2 * RANK, 128), jnp.float32))
    pl.semaphore_wait(barrier, len(partners))

    up = remote(omega.at[bands - 1], ohalo.at[0], halo_s.at[0], halo_r.at[0], tm, next_lon)
    down = remote(omega.at[0], ohalo.at[1], halo_s.at[1], halo_r.at[1], tm, prev_lon)
    f_copies = []
    for d in range(1, NY):
        cols = pl.ds(pl.multiple_of(128 * ((y + d) % NY), 128), 128)
        f_copies.append(
            remote(field.at[:, :, cols], fy.at[d - 1], f_s.at[d - 1], f_r.at[d - 1], y_tms[d - 1], lon)
        )

    def edge_term(side, l):
        tiles = [lat_smooth(ohalo[side, :, c * 128:(c + 1) * 128].astype(jnp.float32)) for c in range(4)]
        return contract_last(halves(jnp.concatenate(tiles, axis=1) * 0.0625), field[l])

    up.wait()
    acc = acc + edge_term(0, 0)
    down.wait()
    acc = acc + edge_term(1, bands - 1)

    cbuf[0] = acc[:RANK] + acc[RANK:]
    copy = remote(cbuf.at[0], cbuf.at[1], core_s, core_r, tm, core_lon)
    copy.wait()
    xbuf[x] = cbuf[0] + cbuf[1]
    copies = [
        remote(xbuf.at[x], xbuf.at[x], x_s.at[i], x_r.at[i], tm, other) for i, other in enumerate(x_lons)
    ]
    for copy in copies:
        copy.wait()
    total = (xbuf[0] + xbuf[1]) + (xbuf[2] + xbuf[3])
    zq[0] = total
    full = remote(zq.at[0], zq.at[1], zq_s, zq_r, tm, zh_lon)
    lane16 = lax.broadcasted_iota(jnp.int32, (16, 128), 1)
    first = jnp.zeros((16, 128), jnp.float32)
    last = jnp.zeros((16, 128), jnp.float32)
    for g in range(4):
        piece = total[16 * g:16 * (g + 1)]
        mine = lane16 // 32 == g
        first = jnp.where(mine, piece if g == 0 else pltpu.roll(piece, 32 * g, 1), first)
        last = jnp.where(mine, piece if g == 3 else pltpu.roll(piece, 32 * (g + 1), 1), last)
    edges[0] = last
    edges[1] = first
    copies = []
    for side, to_tm in ((0, next_tm), (1, prev_tm)):
        for part, to_lon in ((0, lon), (1, zh_lon)):
            i = 2 * side + part
            copies.append(remote(edges.at[side], edge_in.at[i], edge_s.at[i], edge_r.at[i], to_tm, to_lon))
    full.wait()
    for copy in copies:
        copy.wait()
    before = edge_in[0] + edge_in[1]
    after = edge_in[2] + edge_in[3]
    low, high = [], []
    for g in range(4):
        low.append(jnp.where(lane16 >= 96, before if g == 3 else pltpu.roll(before, 96 - 32 * g, 1), 0.0))
        high.append(jnp.where(lane16 < 32, after if g == 0 else pltpu.roll(after, 128 - 32 * g, 1), 0.0))
    has_low = (tm > 0).astype(jnp.float32)
    has_high = (tm < days_blocks - 1).astype(jnp.float32)
    low = jnp.concatenate(low, axis=0) * has_low
    high = jnp.concatenate(high, axis=0) * has_high
    raw = zq[0] + zq[1]

    t_low, t_mid, t_high = (toeplitz[128 * i:128 * (i + 1)] for i in range(3))
    sketch = matmul(low, t_low, HI) + matmul(raw, t_mid, HI) + matmul(high, t_high, HI)
    sketch_low = (matmul(low, t_mid, HI) + matmul(raw, t_high, HI)) * has_low
    sketch_high = (matmul(raw, t_low, HI) + matmul(high, t_mid, HI)) * has_high
    back = matmul(sketch_low, t_low, HI) + matmul(sketch, t_mid, HI) + matmul(sketch_high, t_high, HI)
    ubuf[0] = halves(back)
    u_copies = [
        remote(ubuf.at[0], ubuf.at[d], u_s.at[d - 1], u_r.at[d - 1], y_tms[d - 1], lon) for d in range(1, NY)
    ]
    gram = contract_last(sketch, sketch, HI)
    gbuf[0] = jnp.concatenate([gram, jnp.zeros((RANK, 64), jnp.float32)], axis=1)
    for copy in f_copies + u_copies:
        copy.wait()
    back_all = jnp.concatenate([ubuf[d] for d in range(NY)], axis=1)
    mine = pl.ds(pl.multiple_of(128 * y, 128), 128)

    def pattern_terms(pair, carry):
        blocks = []
        for l in (2 * pair, 2 * pair + 1):
            blocks.append(jnp.concatenate([field[l, :, mine]] + [fy[d, l] for d in range(NY - 1)], axis=0))
        both = matmul(back_all, jnp.concatenate(blocks, axis=1))
        both = both[:RANK] + both[RANK:]
        for k in range(NZ):
            rows = both[8 * k:8 * k + 8]
            zsend[k, pair] = jnp.concatenate([rows[:, :128], rows[:, 128:]], axis=0).astype(jnp.bfloat16)
        return carry

    lax.fori_loop(0, bands // 2, pattern_terms, 0)
    z_copies = []
    for d in range(1, NZ):
        z_copies.append(
            remote(zsend.at[(z + d) % NZ], zrecv.at[d - 1], z_s.at[d - 1], z_r.at[d - 1], z_tms[d - 1], lon)
        )

    steps = [(1, z, 1), (2, z, 2), (4, z, 4), (1, y, NZ), (2, y, 2 * NZ)]
    for i, (bit, coord, stride) in enumerate(steps):
        to_tm = tm + stride - 2 * stride * ((coord // bit) % 2)
        copy = remote(gbuf.at[i], gin.at[i], g_s.at[i], g_r.at[i], to_tm, lon)
        copy.wait()
        gbuf[i + 1] = gbuf[i] + gin[i]

    for copy in z_copies:
        copy.wait()
    value = zsend[z].astype(jnp.float32)
    for d in range(NZ - 1):
        value = value + zrecv[d].astype(jnp.float32)
    value = lat_smooth(value.reshape(bands * 8, 128)) * 0.0625
    lon_edge[0] = value[:8]
    lon_edge[1] = value[bands * 8 - 8:]
    from_high = remote(lon_edge.at[0], lon_in.at[1], le_s.at[0], le_r.at[0], tm, prev_lon)
    from_low = remote(lon_edge.at[1], lon_in.at[0], le_s.at[1], le_r.at[1], tm, next_lon)
    inner = value[8:-24] + 2.0 * value[16:-16] + value[24:-8]
    gathered[y, z] = inner.reshape(bands // 2 - 2, 16, 128).astype(jnp.bfloat16)
    y_next, y_prev = y_tms[0], y_tms[NY - 2]

    def all_z(buf, send, recv):
        return [
            remote(buf.at[y, z], buf.at[y, z], send.at[i], recv.at[i], other, lon) for i, other in enumerate(z_tms)
        ]

    def both_y(buf, send, recv, i):
        k = (z + NZ - i) % NZ
        block = buf.at[y, k]
        return [
            remote(block, block, send.at[i, 0], recv.at[i, 0], y_next, lon),
            remote(block, block, send.at[i, 1], recv.at[i, 1], y_prev, lon),
        ]

    def relay_y(buf, send, recv, i, pair):
        k = (z + NZ - i) % NZ
        way = i % 2
        pair[way].wait_recv()
        block = buf.at[(y + NY - 1) % NY if way == 0 else (y + 1) % NY, k]
        copy = remote(block, block, send.at[i, 2], recv.at[i, 2], y_next if way == 0 else y_prev, lon)
        return [pair[way].wait_send, pair[1 - way].wait, copy.wait]

    az = all_z(gathered, az_s, az_r)
    lane = lax.broadcasted_iota(jnp.int32, (RANK, 128), 1)
    row_of = lax.broadcasted_iota(jnp.int32, (RANK, 128), 0)
    elim[...] = jnp.where(lane == row_of + RANK, 1.0, gbuf[len(steps)])

    def eliminate(j, carry):
        matrix = elim[...]
        row = elim[pl.ds(j, 1), :]
        column = jnp.sum(jnp.where(lane == j, matrix, 0.0), axis=1, keepdims=True)
        pivot = jnp.sum(jnp.where(lane[:1] == j, row, 0.0), axis=1, keepdims=True)
        factor = jnp.where(row_of[:, :1] > j, column / pivot, 0.0)
        elim[...] = matrix - factor * row
        return carry

    order = (0, 1, 7, 2, 6, 3, 5, 4)
    ends = []
    previous = None
    for turn, i in enumerate(order):
        if i:
            az[i - 1].wait_recv()
            ends.append(az[i - 1].wait_send)
        pair = both_y(gathered, ay_s, ay_r, i)
        if previous is not None:
            ends += relay_y(gathered, ay_s, ay_r, *previous)
        previous = (i, pair)
        if turn == 3:
            from_low.wait()
            from_high.wait()
            low_rim = jnp.concatenate([lon_in[0] + 2.0 * value[:8] + value[8:16], value[:8] + 2.0 * value[8:16] + value[16:24]], axis=0)
            high_rim = jnp.concatenate([value[-24:-16] + 2.0 * value[-16:-8] + value[-8:], value[-16:-8] + 2.0 * value[-8:] + lon_in[1]], axis=0)
            rims[y, z] = jnp.stack([low_rim, high_rim]).astype(jnp.bfloat16)
            rz = all_z(rims, rz_s, rz_r)
        lax.fori_loop(8 * turn, 8 * turn + 8, eliminate, 0)
    ends += relay_y(gathered, ay_s, ay_r, *previous)
    pairs = []
    for i in order:
        if i:
            rz[i - 1].wait_recv()
            ends.append(rz[i - 1].wait_send)
        pairs.append((i, both_y(rims, ry_s, ry_r, i)))

    matrix = elim[...]
    diagonal = jnp.sum(jnp.where(lane == row_of, matrix, 0.0), axis=1, keepdims=True)
    inverse = (matrix / jnp.sqrt(diagonal))[:, RANK:]
    basis = matmul(inverse, sketch, HI)
    series_out[...] = basis * math.sqrt(128 * days_blocks)
    basis_out[...] = contract_first(basis, inverse, HI).astype(jnp.bfloat16)

    for i, pair in pairs:
        ends += relay_y(rims, ry_s, ry_r, i, pair)
    for end in ends:
        end()

    def unpack_pair(source, at, pair):
        for c in range(NY):
            both = [source[c, k, at].astype(jnp.float32) for k in range(NZ)]
            cols = slice(128 * c, 128 * c + 128)
            for i in range(2):
                rows = jnp.concatenate([block[8 * i:8 * i + 8] for block in both], axis=0)
                patterns_out[2 * pair + i, :, cols] = rows.astype(jnp.bfloat16)

    def unpack(pair, carry):
        unpack_pair(gathered, pair - 1, pair)
        return carry

    lax.fori_loop(1, bands // 2 - 1, unpack, 0)
    unpack_pair(rims, 0, 0)
    unpack_pair(rims, 1, bands // 2 - 1)


def project(basis, patterns, out):
    for i in range(patterns.shape[0]):
        out[i] = matmul(basis[...], patterns[i]).astype(jnp.bfloat16)


def local(field, omega):
    days, bands, cols = field.shape
    pairs = bands // 2
    f32, bf16 = jnp.float32, jnp.bfloat16
    dma = pltpu.SemaphoreType.DMA
    vmem = pl.BlockSpec(memory_space=pltpu.VMEM)
    patterns, basis, series = pl.pallas_call(
        kernel,
        out_shape=(
            jax.ShapeDtypeStruct((bands, RANK, cols), bf16),
            jax.ShapeDtypeStruct((days, RANK), bf16),
            jax.ShapeDtypeStruct((RANK, days), f32),
        ),
        in_specs=[vmem] * 3,
        out_specs=(vmem,) * 3,
        scratch_shapes=[
            pltpu.VMEM((2, RANK, cols), bf16),
            pltpu.VMEM((bands + 2, RANK, cols), f32),
            pltpu.VMEM((NY - 1, bands, days, 128), bf16),
            pltpu.VMEM((NY, 2 * RANK, days), bf16),
            pltpu.VMEM((2, RANK, days), f32),
            pltpu.VMEM((NX, RANK, days), f32),
            pltpu.VMEM((2, RANK, days), f32),
            pltpu.VMEM((2, 16, days), f32),
            pltpu.VMEM((4, 16, days), f32),
            pltpu.VMEM((6, RANK, 128), f32),
            pltpu.VMEM((5, RANK, 128), f32),
            pltpu.VMEM((NZ, pairs, 16, 128), bf16),
            pltpu.VMEM((NZ - 1, pairs, 16, 128), bf16),
            pltpu.VMEM((2, 8, 128), f32),
            pltpu.VMEM((2, 8, 128), f32),
            pltpu.VMEM((NY, NZ, pairs - 2, 16, 128), bf16),
            pltpu.VMEM((NY, NZ, 2, 16, 128), bf16),
            pltpu.VMEM((RANK, 128), f32),
            dma((2,)), dma((2,)), dma, dma, dma((3,)), dma((3,)), dma, dma, dma((4,)), dma((4,)),
            dma((5,)), dma((5,)), dma((3,)), dma((3,)), dma((3,)), dma((3,)), dma((7,)), dma((7,)),
            dma((2,)), dma((2,)), dma((7,)), dma((7,)), dma((8, 3)), dma((8, 3)),
            dma((7,)), dma((7,)), dma((8, 3)), dma((8, 3)),
        ],
        compiler_params=pltpu.CompilerParams(collective_id=0, has_side_effects=True),
        name="subspace",
    )(jnp.transpose(field, (1, 0, 2)), jnp.transpose(omega, (0, 2, 1)), jnp.asarray(toeplitz_blocks()))
    step = 3
    projected = pl.pallas_call(
        project,
        grid=(bands // step,),
        out_shape=jax.ShapeDtypeStruct((bands, days, cols), bf16),
        in_specs=[
            pl.BlockSpec((days, RANK), lambda i: (0, 0)),
            pl.BlockSpec((step, RANK, cols), lambda i: (i, 0, 0)),
        ],
        out_specs=pl.BlockSpec((step, days, cols), lambda i: (i, 0, 0)),
        name="project",
    )(basis, patterns)
    return jnp.transpose(projected, (1, 0, 2)), series.T


def solution(mesh):
    in_specs = (P("tm", "lon", None), P("lon", None, None))
    out_specs = (P("tm", "lon", None), P("tm", None))
    return jax.shard_map(local, mesh=mesh, in_specs=in_specs, out_specs=out_specs, check_vma=False)
```

```python
import math

import jax
import jax.numpy as jnp
import ml_dtypes
import numpy as np
from jax import lax
from jax.experimental import pallas as pl
from jax.experimental.pallas import tpu as pltpu
from jax.sharding import PartitionSpec as P

NLAT = 32
HALF = 15
RANK = 64
NY, NZ, NX = 4, 8, 4
HI = lax.Precision.HIGHEST
MESH = pl.DeviceIdType.MESH


def toeplitz_blocks():
    offsets = np.arange(-HALF, HALF + 1).astype(np.float64)
    safe = np.where(offsets == 0, 1.0, offsets)
    core = (np.sin(2.0 * math.pi * safe / 3.0) - np.sin(2.0 * math.pi * safe / 30.0)) / (math.pi * safe)
    core = np.where(offsets == 0, 2.0 * (1.0 / 3.0 - 1.0 / 30.0), core)
    spread = math.pi * safe / (HALF + 1)
    sigma = np.where(offsets == 0, 1.0, np.sin(spread) / spread)
    taps = (core * sigma).astype(np.float32).astype(ml_dtypes.bfloat16).astype(np.float32)
    rows = np.arange(384)[:, None] - 128
    cols = np.arange(128)[None, :]
    diff = rows - cols
    inside = np.abs(diff) <= HALF
    return np.where(inside, taps[np.clip(diff + HALF, 0, 2 * HALF)], 0.0).astype(np.float32)


def halves(value):
    high = value.astype(jnp.bfloat16)
    low = (value - high.astype(jnp.float32)).astype(jnp.bfloat16)
    return jnp.concatenate([high, low], axis=0)


def contract_last(a, b, precision=None):
    return lax.dot_general(a, b, (((1,), (1,)), ((), ())), precision=precision, preferred_element_type=jnp.float32)


def contract_first(a, b, precision=None):
    return lax.dot_general(a, b, (((0,), (0,)), ((), ())), precision=precision, preferred_element_type=jnp.float32)


def matmul(a, b, precision=None):
    return jnp.dot(a, b, precision=precision, preferred_element_type=jnp.float32)


def lat_smooth(tile):
    lane = lax.broadcasted_iota(jnp.int32, tile.shape, tile.ndim - 1) % NLAT
    left = jnp.where(lane == 0, 0.0, pltpu.roll(tile, 1, tile.ndim - 1))
    right = jnp.where(lane == NLAT - 1, 0.0, pltpu.roll(tile, 127, tile.ndim - 1))
    return left + 2.0 * tile + right


def kernel(
    field, omega, toeplitz, patterns_out, basis_out, series_out,
    ohalo, osm, fy, ubuf, cbuf, xbuf, zq, edges, edge_in, gz, gy, zsend, zrecv, lon_edge, lon_in, gathered, rims, elim,
    halo_s, halo_r, core_s, core_r, x_s, x_r, zq_s, zq_r, edge_s, edge_r, gz_s, gz_r, gy_s, gy_r, f_s, f_r, u_s, u_r, z_s, z_r,
    le_s, le_r, az_s, az_r, ay_s, ay_r, rz_s, rz_r, ry_s, ry_r,
):
    bands = field.shape[0]
    tm = lax.axis_index("tm")
    lon = lax.axis_index("lon")
    days_blocks = NY * NZ
    y, z = tm // NZ, tm % NZ
    nlon = 16
    next_lon, prev_lon = (lon + 1) % nlon, (lon + nlon - 1) % nlon
    core_lon = lon + 1 - 2 * (lon % 2)
    zh_lon = lon + 2 - 4 * ((lon // 2) % 2)
    x = lon // 4
    x_lons = [((x + d) % NX) * 4 + lon % 4 for d in range(1, NX)]
    next_tm, prev_tm = (tm + 1) % days_blocks, (tm + days_blocks - 1) % days_blocks
    y_tms = [((y + d) % NY) * NZ + z for d in range(1, NY)]
    z_tms = [y * NZ + (z + d) % NZ for d in range(1, NZ)]

    def remote(src, dst, send, recv, to_tm, to_lon):
        copy = pltpu.make_async_remote_copy(
            src_ref=src, dst_ref=dst, send_sem=send, recv_sem=recv,
            device_id=(to_tm, to_lon), device_id_type=MESH,
        )
        copy.start()
        return copy

    barrier = pltpu.get_barrier_semaphore()
    partners = [(tm, next_lon), (tm, prev_lon), (tm, zh_lon)]
    partners += [(tm, other) for other in x_lons]
    partners += [(t, l) for t in (next_tm, prev_tm) for l in (lon, zh_lon)]
    partners += [(t, lon) for t in y_tms + z_tms]
    for partner in partners:
        pl.semaphore_signal(barrier, inc=1, device_id=partner, device_id_type=MESH)

    osm[0] = jnp.zeros_like(osm[0])
    osm[bands + 1] = jnp.zeros_like(osm[0])

    def smooth_omega(l, carry):
        for c in range(4):
            tile = omega[l, :, c * 128:(c + 1) * 128].astype(jnp.float32)
            osm[l + 1, :, c * 128:(c + 1) * 128] = lat_smooth(tile) * 0.0625
        return carry

    lax.fori_loop(0, bands, smooth_omega, 0)

    def sketch_term(l, acc):
        weights = osm[l] + 2.0 * osm[l + 1] + osm[l + 2]
        return acc + contract_last(halves(weights), field[l])

    acc = lax.fori_loop(0, bands, sketch_term, jnp.zeros((2 * RANK, 128), jnp.float32))
    pl.semaphore_wait(barrier, len(partners))

    up = remote(omega.at[bands - 1], ohalo.at[0], halo_s.at[0], halo_r.at[0], tm, next_lon)
    down = remote(omega.at[0], ohalo.at[1], halo_s.at[1], halo_r.at[1], tm, prev_lon)
    f_copies = []
    for d in range(1, NY):
        cols = pl.ds(pl.multiple_of(128 * ((y + d) % NY), 128), 128)
        f_copies.append(
            remote(field.at[:, :, cols], fy.at[d - 1], f_s.at[d - 1], f_r.at[d - 1], y_tms[d - 1], lon)
        )

    def edge_term(side, l):
        tiles = [lat_smooth(ohalo[side, :, c * 128:(c + 1) * 128].astype(jnp.float32)) for c in range(4)]
        return contract_last(halves(jnp.concatenate(tiles, axis=1) * 0.0625), field[l])

    up.wait()
    acc = acc + edge_term(0, 0)
    down.wait()
    acc = acc + edge_term(1, bands - 1)

    cbuf[0] = acc[:RANK] + acc[RANK:]
    copy = remote(cbuf.at[0], cbuf.at[1], core_s, core_r, tm, core_lon)
    copy.wait()
    xbuf[x] = cbuf[0] + cbuf[1]
    copies = [
        remote(xbuf.at[x], xbuf.at[x], x_s.at[i], x_r.at[i], tm, other) for i, other in enumerate(x_lons)
    ]
    for copy in copies:
        copy.wait()
    total = (xbuf[0] + xbuf[1]) + (xbuf[2] + xbuf[3])
    zq[0] = total
    full = remote(zq.at[0], zq.at[1], zq_s, zq_r, tm, zh_lon)
    lane16 = lax.broadcasted_iota(jnp.int32, (16, 128), 1)
    first = jnp.zeros((16, 128), jnp.float32)
    last = jnp.zeros((16, 128), jnp.float32)
    for g in range(4):
        piece = total[16 * g:16 * (g + 1)]
        mine = lane16 // 32 == g
        first = jnp.where(mine, piece if g == 0 else pltpu.roll(piece, 32 * g, 1), first)
        last = jnp.where(mine, piece if g == 3 else pltpu.roll(piece, 32 * (g + 1), 1), last)
    edges[0] = last
    edges[1] = first
    copies = []
    for side, to_tm in ((0, next_tm), (1, prev_tm)):
        for part, to_lon in ((0, lon), (1, zh_lon)):
            i = 2 * side + part
            copies.append(remote(edges.at[side], edge_in.at[i], edge_s.at[i], edge_r.at[i], to_tm, to_lon))
    full.wait()
    for copy in copies:
        copy.wait()
    before = edge_in[0] + edge_in[1]
    after = edge_in[2] + edge_in[3]
    low, high = [], []
    for g in range(4):
        low.append(jnp.where(lane16 >= 96, before if g == 3 else pltpu.roll(before, 96 - 32 * g, 1), 0.0))
        high.append(jnp.where(lane16 < 32, after if g == 0 else pltpu.roll(after, 128 - 32 * g, 1), 0.0))
    has_low = (tm > 0).astype(jnp.float32)
    has_high = (tm < days_blocks - 1).astype(jnp.float32)
    low = jnp.concatenate(low, axis=0) * has_low
    high = jnp.concatenate(high, axis=0) * has_high
    raw = zq[0] + zq[1]

    t_low, t_mid, t_high = (toeplitz[128 * i:128 * (i + 1)] for i in range(3))
    sketch = matmul(low, t_low, HI) + matmul(raw, t_mid, HI) + matmul(high, t_high, HI)
    sketch_low = (matmul(low, t_mid, HI) + matmul(raw, t_high, HI)) * has_low
    sketch_high = (matmul(raw, t_low, HI) + matmul(high, t_mid, HI)) * has_high
    back = matmul(sketch_low, t_low, HI) + matmul(sketch, t_mid, HI) + matmul(sketch_high, t_high, HI)
    gram = contract_last(sketch, sketch, HI)
    gz[z] = jnp.concatenate([gram[:32], gram[32:]], axis=1)
    gz_copies = [
        remote(gz.at[z], gz.at[z], gz_s.at[i], gz_r.at[i], other, lon) for i, other in enumerate(z_tms)
    ]
    ubuf[0] = halves(back)
    u_copies = [
        remote(ubuf.at[0], ubuf.at[d], u_s.at[d - 1], u_r.at[d - 1], y_tms[d - 1], lon) for d in range(1, NY)
    ]
    for copy in f_copies + u_copies:
        copy.wait()
    back_all = jnp.concatenate([ubuf[d] for d in range(NY)], axis=1)
    mine = pl.ds(pl.multiple_of(128 * y, 128), 128)

    def pattern_terms(pair, carry):
        blocks = []
        for l in (2 * pair, 2 * pair + 1):
            blocks.append(jnp.concatenate([field[l, :, mine]] + [fy[d, l] for d in range(NY - 1)], axis=0))
        both = matmul(back_all, jnp.concatenate(blocks, axis=1))
        both = both[:RANK] + both[RANK:]
        for k in range(NZ):
            rows = both[8 * k:8 * k + 8]
            zsend[k, pair] = jnp.concatenate([rows[:, :128], rows[:, 128:]], axis=0).astype(jnp.bfloat16)
        return carry

    lax.fori_loop(0, bands // 2, pattern_terms, 0)
    z_copies = []
    for d in range(1, NZ):
        z_copies.append(
            remote(zsend.at[(z + d) % NZ], zrecv.at[d - 1], z_s.at[d - 1], z_r.at[d - 1], z_tms[d - 1], lon)
        )

    for copy in gz_copies:
        copy.wait()
    part = gz[0]
    for k in range(1, NZ):
        part = part + gz[k]
    gy[y] = part
    gy_copies = [
        remote(gy.at[y], gy.at[y], gy_s.at[i], gy_r.at[i], other, lon) for i, other in enumerate(y_tms)
    ]
    for copy in gy_copies:
        copy.wait()
    part = (gy[0] + gy[1]) + (gy[2] + gy[3])
    lane = lax.broadcasted_iota(jnp.int32, (RANK, 128), 1)
    row_of = lax.broadcasted_iota(jnp.int32, (RANK, 128), 0)
    stacked = jnp.concatenate([part, pltpu.roll(part, 64, 1)], axis=0)
    elim[...] = jnp.where(lane < RANK, stacked, jnp.where(lane == row_of + RANK, 1.0, 0.0))

    def eliminate(j, carry):
        matrix = elim[...]
        row = elim[pl.ds(j, 1), :]
        column = jnp.sum(jnp.where(lane == j, matrix, 0.0), axis=1, keepdims=True)
        pivot = jnp.sum(jnp.where(lane[:1] == j, row, 0.0), axis=1, keepdims=True)
        factor = jnp.where(row_of[:, :1] > j, column / pivot, 0.0)
        elim[...] = matrix - factor * row
        return carry

    lax.fori_loop(0, RANK, eliminate, 0)

    for copy in z_copies:
        copy.wait()
    value = zsend[z].astype(jnp.float32)
    for d in range(NZ - 1):
        value = value + zrecv[d].astype(jnp.float32)
    value = lat_smooth(value.reshape(bands * 8, 128)) * 0.0625
    lon_edge[0] = value[:8]
    lon_edge[1] = value[bands * 8 - 8:]
    from_high = remote(lon_edge.at[0], lon_in.at[1], le_s.at[0], le_r.at[0], tm, prev_lon)
    from_low = remote(lon_edge.at[1], lon_in.at[0], le_s.at[1], le_r.at[1], tm, next_lon)
    inner = value[8:-24] + 2.0 * value[16:-16] + value[24:-8]
    gathered[y, z] = inner.reshape(bands // 2 - 2, 16, 128).astype(jnp.bfloat16)
    y_next, y_prev = y_tms[0], y_tms[NY - 2]

    def all_z(buf, send, recv):
        return [
            remote(buf.at[y, z], buf.at[y, z], send.at[i], recv.at[i], other, lon) for i, other in enumerate(z_tms)
        ]

    def both_y(buf, send, recv, i):
        k = (z + NZ - i) % NZ
        block = buf.at[y, k]
        return [
            remote(block, block, send.at[i, 0], recv.at[i, 0], y_next, lon),
            remote(block, block, send.at[i, 1], recv.at[i, 1], y_prev, lon),
        ]

    def relay_y(buf, send, recv, i, pair):
        k = (z + NZ - i) % NZ
        way = i % 2
        pair[way].wait_recv()
        block = buf.at[(y + NY - 1) % NY if way == 0 else (y + 1) % NY, k]
        copy = remote(block, block, send.at[i, 2], recv.at[i, 2], y_next if way == 0 else y_prev, lon)
        return [pair[way].wait_send, pair[1 - way].wait, copy.wait]

    az = all_z(gathered, az_s, az_r)
    order = (0, 1, 7, 2, 6, 3, 5, 4)
    ends = []
    previous = None
    for turn, i in enumerate(order):
        if i:
            az[i - 1].wait_recv()
            ends.append(az[i - 1].wait_send)
        pair = both_y(gathered, ay_s, ay_r, i)
        if previous is not None:
            ends += relay_y(gathered, ay_s, ay_r, *previous)
        previous = (i, pair)
        if turn == 5:
            from_low.wait()
            from_high.wait()
            low_rim = jnp.concatenate([lon_in[0] + 2.0 * value[:8] + value[8:16], value[:8] + 2.0 * value[8:16] + value[16:24]], axis=0)
            high_rim = jnp.concatenate([value[-24:-16] + 2.0 * value[-16:-8] + value[-8:], value[-16:-8] + 2.0 * value[-8:] + lon_in[1]], axis=0)
            rims[y, z] = jnp.stack([low_rim, high_rim]).astype(jnp.bfloat16)
            rz = all_z(rims, rz_s, rz_r)
    ends += relay_y(gathered, ay_s, ay_r, *previous)
    pairs = []
    for i in order:
        if i:
            rz[i - 1].wait_recv()
            ends.append(rz[i - 1].wait_send)
        pairs.append((i, both_y(rims, ry_s, ry_r, i)))

    matrix = elim[...]
    diagonal = jnp.sum(jnp.where(lane == row_of, matrix, 0.0), axis=1, keepdims=True)
    inverse = (matrix / jnp.sqrt(diagonal))[:, RANK:]
    basis = matmul(inverse, sketch, HI)
    series_out[...] = basis * math.sqrt(128 * days_blocks)
    basis_out[...] = contract_first(basis, inverse, HI).astype(jnp.bfloat16)

    for i, pair in pairs:
        ends += relay_y(rims, ry_s, ry_r, i, pair)
    for end in ends:
        end()

    def unpack_pair(source, at, pair):
        for c in range(NY):
            both = [source[c, k, at].astype(jnp.float32) for k in range(NZ)]
            cols = slice(128 * c, 128 * c + 128)
            for i in range(2):
                rows = jnp.concatenate([block[8 * i:8 * i + 8] for block in both], axis=0)
                patterns_out[2 * pair + i, :, cols] = rows.astype(jnp.bfloat16)

    def unpack(pair, carry):
        unpack_pair(gathered, pair - 1, pair)
        return carry

    lax.fori_loop(1, bands // 2 - 1, unpack, 0)
    unpack_pair(rims, 0, 0)
    unpack_pair(rims, 1, bands // 2 - 1)


def project(basis, patterns, out):
    for i in range(patterns.shape[0]):
        out[i] = matmul(basis[...], patterns[i]).astype(jnp.bfloat16)


def local(field, omega):
    days, bands, cols = field.shape
    pairs = bands // 2
    f32, bf16 = jnp.float32, jnp.bfloat16
    dma = pltpu.SemaphoreType.DMA
    vmem = pl.BlockSpec(memory_space=pltpu.VMEM)
    patterns, basis, series = pl.pallas_call(
        kernel,
        out_shape=(
            jax.ShapeDtypeStruct((bands, RANK, cols), bf16),
            jax.ShapeDtypeStruct((days, RANK), bf16),
            jax.ShapeDtypeStruct((RANK, days), f32),
        ),
        in_specs=[vmem] * 3,
        out_specs=(vmem,) * 3,
        scratch_shapes=[
            pltpu.VMEM((2, RANK, cols), bf16),
            pltpu.VMEM((bands + 2, RANK, cols), f32),
            pltpu.VMEM((NY - 1, bands, days, 128), bf16),
            pltpu.VMEM((NY, 2 * RANK, days), bf16),
            pltpu.VMEM((2, RANK, days), f32),
            pltpu.VMEM((NX, RANK, days), f32),
            pltpu.VMEM((2, RANK, days), f32),
            pltpu.VMEM((2, 16, days), f32),
            pltpu.VMEM((4, 16, days), f32),
            pltpu.VMEM((NZ, 32, 128), f32),
            pltpu.VMEM((NY, 32, 128), f32),
            pltpu.VMEM((NZ, pairs, 16, 128), bf16),
            pltpu.VMEM((NZ - 1, pairs, 16, 128), bf16),
            pltpu.VMEM((2, 8, 128), f32),
            pltpu.VMEM((2, 8, 128), f32),
            pltpu.VMEM((NY, NZ, pairs - 2, 16, 128), bf16),
            pltpu.VMEM((NY, NZ, 2, 16, 128), bf16),
            pltpu.VMEM((RANK, 128), f32),
            dma((2,)), dma((2,)), dma, dma, dma((3,)), dma((3,)), dma, dma, dma((4,)), dma((4,)),
            dma((7,)), dma((7,)), dma((3,)), dma((3,)), dma((3,)), dma((3,)), dma((3,)), dma((3,)), dma((7,)), dma((7,)),
            dma((2,)), dma((2,)), dma((7,)), dma((7,)), dma((8, 3)), dma((8, 3)),
            dma((7,)), dma((7,)), dma((8, 3)), dma((8, 3)),
        ],
        compiler_params=pltpu.CompilerParams(collective_id=0, has_side_effects=True),
        name="subspace",
    )(jnp.transpose(field, (1, 0, 2)), jnp.transpose(omega, (0, 2, 1)), jnp.asarray(toeplitz_blocks()))
    step = 3
    projected = pl.pallas_call(
        project,
        grid=(bands // step,),
        out_shape=jax.ShapeDtypeStruct((bands, days, cols), bf16),
        in_specs=[
            pl.BlockSpec((days, RANK), lambda i: (0, 0)),
            pl.BlockSpec((step, RANK, cols), lambda i: (i, 0, 0)),
        ],
        out_specs=pl.BlockSpec((step, days, cols), lambda i: (i, 0, 0)),
        name="project",
    )(basis, patterns)
    return jnp.transpose(projected, (1, 0, 2)), series.T


def solution(mesh):
    in_specs = (P("tm", "lon", None), P("lon", None, None))
    out_specs = (P("tm", "lon", None), P("tm", None))
    return jax.shard_map(local, mesh=mesh, in_specs=in_specs, out_specs=out_specs, check_vma=False)
```

```python
import math

import jax
import jax.numpy as jnp
import ml_dtypes
import numpy as np
from jax import lax
from jax.experimental import pallas as pl
from jax.experimental.pallas import tpu as pltpu
from jax.sharding import PartitionSpec as P

NLAT = 32
HALF = 15
RANK = 64
NY, NZ, NX = 4, 8, 4
HI = lax.Precision.HIGHEST
MESH = pl.DeviceIdType.MESH


def toeplitz_blocks():
    offsets = np.arange(-HALF, HALF + 1).astype(np.float64)
    safe = np.where(offsets == 0, 1.0, offsets)
    core = (np.sin(2.0 * math.pi * safe / 3.0) - np.sin(2.0 * math.pi * safe / 30.0)) / (math.pi * safe)
    core = np.where(offsets == 0, 2.0 * (1.0 / 3.0 - 1.0 / 30.0), core)
    spread = math.pi * safe / (HALF + 1)
    sigma = np.where(offsets == 0, 1.0, np.sin(spread) / spread)
    taps = (core * sigma).astype(np.float32).astype(ml_dtypes.bfloat16).astype(np.float32)
    rows = np.arange(384)[:, None] - 128
    cols = np.arange(128)[None, :]
    diff = rows - cols
    inside = np.abs(diff) <= HALF
    return np.where(inside, taps[np.clip(diff + HALF, 0, 2 * HALF)], 0.0).astype(np.float32)


def halves(value):
    high = value.astype(jnp.bfloat16)
    low = (value - high.astype(jnp.float32)).astype(jnp.bfloat16)
    return jnp.concatenate([high, low], axis=0)


def contract_last(a, b, precision=None):
    return lax.dot_general(a, b, (((1,), (1,)), ((), ())), precision=precision, preferred_element_type=jnp.float32)


def contract_first(a, b, precision=None):
    return lax.dot_general(a, b, (((0,), (0,)), ((), ())), precision=precision, preferred_element_type=jnp.float32)


def matmul(a, b, precision=None):
    return jnp.dot(a, b, precision=precision, preferred_element_type=jnp.float32)


def lat_smooth(tile):
    lane = lax.broadcasted_iota(jnp.int32, tile.shape, tile.ndim - 1) % NLAT
    left = jnp.where(lane == 0, 0.0, pltpu.roll(tile, 1, tile.ndim - 1))
    right = jnp.where(lane == NLAT - 1, 0.0, pltpu.roll(tile, 127, tile.ndim - 1))
    return left + 2.0 * tile + right


def kernel(
    field, omega, toeplitz, patterns_out, basis_out, series_out,
    ohalo, osm, fy, ubuf, cbuf, xbuf, zq, edges, edge_in, gz, gy, zsend, zrecv, lon_edge, lon_in, gathered, rims, elim,
    halo_s, halo_r, core_s, core_r, x_s, x_r, zq_s, zq_r, edge_s, edge_r, gz_s, gz_r, gy_s, gy_r, f_s, f_r, u_s, u_r, z_s, z_r,
    le_s, le_r, az_s, az_r, ay_s, ay_r, rz_s, rz_r, ry_s, ry_r,
):
    bands = field.shape[0]
    tm = lax.axis_index("tm")
    lon = lax.axis_index("lon")
    days_blocks = NY * NZ
    y, z = tm // NZ, tm % NZ
    nlon = 16
    next_lon, prev_lon = (lon + 1) % nlon, (lon + nlon - 1) % nlon
    core_lon = lon + 1 - 2 * (lon % 2)
    zh_lon = lon + 2 - 4 * ((lon // 2) % 2)
    x = lon // 4
    x_lons = [((x + d) % NX) * 4 + lon % 4 for d in range(1, NX)]
    next_tm, prev_tm = (tm + 1) % days_blocks, (tm + days_blocks - 1) % days_blocks
    y_tms = [((y + d) % NY) * NZ + z for d in range(1, NY)]
    z_tms = [y * NZ + (z + d) % NZ for d in range(1, NZ)]

    def remote(src, dst, send, recv, to_tm, to_lon):
        copy = pltpu.make_async_remote_copy(
            src_ref=src, dst_ref=dst, send_sem=send, recv_sem=recv,
            device_id=(to_tm, to_lon), device_id_type=MESH,
        )
        copy.start()
        return copy

    barrier = pltpu.get_barrier_semaphore()
    partners = [(tm, next_lon), (tm, prev_lon), (tm, zh_lon)]
    partners += [(tm, other) for other in x_lons]
    partners += [(t, l) for t in (next_tm, prev_tm) for l in (lon, zh_lon)]
    partners += [(t, lon) for t in y_tms + z_tms]
    for partner in partners:
        pl.semaphore_signal(barrier, inc=1, device_id=partner, device_id_type=MESH)

    osm[0] = jnp.zeros_like(osm[0])
    osm[bands + 1] = jnp.zeros_like(osm[0])

    def smooth_omega(l, carry):
        for c in range(4):
            tile = omega[l, :, c * 128:(c + 1) * 128].astype(jnp.float32)
            osm[l + 1, :, c * 128:(c + 1) * 128] = lat_smooth(tile) * 0.0625
        return carry

    lax.fori_loop(0, bands, smooth_omega, 0)

    def sketch_term(l, acc):
        weights = osm[l] + 2.0 * osm[l + 1] + osm[l + 2]
        return acc + contract_last(halves(weights), field[l])

    acc = lax.fori_loop(0, bands, sketch_term, jnp.zeros((2 * RANK, 128), jnp.float32))
    pl.semaphore_wait(barrier, len(partners))

    up = remote(omega.at[bands - 1], ohalo.at[0], halo_s.at[0], halo_r.at[0], tm, next_lon)
    down = remote(omega.at[0], ohalo.at[1], halo_s.at[1], halo_r.at[1], tm, prev_lon)
    f_copies = []
    for d in range(1, NY):
        cols = pl.ds(pl.multiple_of(128 * ((y + d) % NY), 128), 128)
        f_copies.append(
            remote(field.at[:, :, cols], fy.at[d - 1], f_s.at[d - 1], f_r.at[d - 1], y_tms[d - 1], lon)
        )

    def edge_term(side, l):
        tiles = [lat_smooth(ohalo[side, :, c * 128:(c + 1) * 128].astype(jnp.float32)) for c in range(4)]
        return contract_last(halves(jnp.concatenate(tiles, axis=1) * 0.0625), field[l])

    up.wait()
    acc = acc + edge_term(0, 0)
    down.wait()
    acc = acc + edge_term(1, bands - 1)

    cbuf[0] = acc[:RANK] + acc[RANK:]
    copy = remote(cbuf.at[0], cbuf.at[1], core_s, core_r, tm, core_lon)
    copy.wait()
    xbuf[x] = cbuf[0] + cbuf[1]
    copies = [
        remote(xbuf.at[x], xbuf.at[x], x_s.at[i], x_r.at[i], tm, other) for i, other in enumerate(x_lons)
    ]
    for copy in copies:
        copy.wait()
    total = (xbuf[0] + xbuf[1]) + (xbuf[2] + xbuf[3])
    zq[0] = total
    full = remote(zq.at[0], zq.at[1], zq_s, zq_r, tm, zh_lon)
    lane16 = lax.broadcasted_iota(jnp.int32, (16, 128), 1)
    first = jnp.zeros((16, 128), jnp.float32)
    last = jnp.zeros((16, 128), jnp.float32)
    for g in range(4):
        piece = total[16 * g:16 * (g + 1)]
        mine = lane16 // 32 == g
        first = jnp.where(mine, piece if g == 0 else pltpu.roll(piece, 32 * g, 1), first)
        last = jnp.where(mine, piece if g == 3 else pltpu.roll(piece, 32 * (g + 1), 1), last)
    edges[0] = last
    edges[1] = first
    copies = []
    for side, to_tm in ((0, next_tm), (1, prev_tm)):
        for part, to_lon in ((0, lon), (1, zh_lon)):
            i = 2 * side + part
            copies.append(remote(edges.at[side], edge_in.at[i], edge_s.at[i], edge_r.at[i], to_tm, to_lon))
    full.wait()
    for copy in copies:
        copy.wait()
    before = edge_in[0] + edge_in[1]
    after = edge_in[2] + edge_in[3]
    low, high = [], []
    for g in range(4):
        low.append(jnp.where(lane16 >= 96, before if g == 3 else pltpu.roll(before, 96 - 32 * g, 1), 0.0))
        high.append(jnp.where(lane16 < 32, after if g == 0 else pltpu.roll(after, 128 - 32 * g, 1), 0.0))
    has_low = (tm > 0).astype(jnp.float32)
    has_high = (tm < days_blocks - 1).astype(jnp.float32)
    low = jnp.concatenate(low, axis=0) * has_low
    high = jnp.concatenate(high, axis=0) * has_high
    raw = zq[0] + zq[1]

    t_low, t_mid, t_high = (toeplitz[128 * i:128 * (i + 1)] for i in range(3))
    sketch = matmul(low, t_low, HI) + matmul(raw, t_mid, HI) + matmul(high, t_high, HI)
    sketch_low = (matmul(low, t_mid, HI) + matmul(raw, t_high, HI)) * has_low
    sketch_high = (matmul(raw, t_low, HI) + matmul(high, t_mid, HI)) * has_high
    back = matmul(sketch_low, t_low, HI) + matmul(sketch, t_mid, HI) + matmul(sketch_high, t_high, HI)
    gram = contract_last(sketch, sketch, HI)
    gz[z] = jnp.concatenate([gram[:32], gram[32:]], axis=1)
    gz_copies = [
        remote(gz.at[z], gz.at[z], gz_s.at[i], gz_r.at[i], other, lon) for i, other in enumerate(z_tms)
    ]
    ubuf[0] = halves(back)
    u_copies = [
        remote(ubuf.at[0], ubuf.at[d], u_s.at[d - 1], u_r.at[d - 1], y_tms[d - 1], lon) for d in range(1, NY)
    ]
    for copy in f_copies + u_copies:
        copy.wait()
    back_all = jnp.concatenate([ubuf[d] for d in range(NY)], axis=1)
    mine = pl.ds(pl.multiple_of(128 * y, 128), 128)

    def pattern_terms(pair, carry):
        blocks = []
        for l in (2 * pair, 2 * pair + 1):
            blocks.append(jnp.concatenate([field[l, :, mine]] + [fy[d, l] for d in range(NY - 1)], axis=0))
        both = matmul(back_all, jnp.concatenate(blocks, axis=1))
        both = both[:RANK] + both[RANK:]
        for k in range(NZ):
            rows = both[8 * k:8 * k + 8]
            zsend[k, pair] = jnp.concatenate([rows[:, :128], rows[:, 128:]], axis=0).astype(jnp.bfloat16)
        return carry

    lax.fori_loop(0, bands // 2, pattern_terms, 0)
    z_copies = []
    for d in range(1, NZ):
        z_copies.append(
            remote(zsend.at[(z + d) % NZ], zrecv.at[d - 1], z_s.at[d - 1], z_r.at[d - 1], z_tms[d - 1], lon)
        )

    for copy in gz_copies:
        copy.wait()
    part = gz[0]
    for k in range(1, NZ):
        part = part + gz[k]
    gy[y] = part
    gy_copies = [
        remote(gy.at[y], gy.at[y], gy_s.at[i], gy_r.at[i], other, lon) for i, other in enumerate(y_tms)
    ]
    for copy in gy_copies:
        copy.wait()
    part = (gy[0] + gy[1]) + (gy[2] + gy[3])
    lane = lax.broadcasted_iota(jnp.int32, (RANK, 128), 1)
    row_of = lax.broadcasted_iota(jnp.int32, (RANK, 128), 0)
    stacked = jnp.concatenate([part, pltpu.roll(part, 64, 1)], axis=0)
    elim[...] = jnp.where(lane < RANK, stacked, jnp.where(lane == row_of + RANK, 1.0, 0.0))

    def eliminate(j, carry):
        matrix = elim[...]
        row = elim[pl.ds(j, 1), :]
        column = jnp.sum(jnp.where(lane == j, matrix, 0.0), axis=1, keepdims=True)
        pivot = jnp.sum(jnp.where(lane[:1] == j, row, 0.0), axis=1, keepdims=True)
        factor = jnp.where(row_of[:, :1] > j, column / pivot, 0.0)
        elim[...] = matrix - factor * row
        return carry

    lax.fori_loop(0, RANK, eliminate, 0)

    for copy in z_copies:
        copy.wait()
    value = zsend[z].astype(jnp.float32)
    for d in range(NZ - 1):
        value = value + zrecv[d].astype(jnp.float32)
    value = lat_smooth(value.reshape(bands * 8, 128)) * 0.0625
    lon_edge[0] = value[:8]
    lon_edge[1] = value[bands * 8 - 8:]
    from_high = remote(lon_edge.at[0], lon_in.at[1], le_s.at[0], le_r.at[0], tm, prev_lon)
    from_low = remote(lon_edge.at[1], lon_in.at[0], le_s.at[1], le_r.at[1], tm, next_lon)
    inner = value[8:-24] + 2.0 * value[16:-16] + value[24:-8]
    gathered[y, z] = inner.reshape(bands // 2 - 2, 16, 128).astype(jnp.bfloat16)
    y_next, y_prev = y_tms[0], y_tms[NY - 2]

    def all_z(buf, send, recv):
        return [
            remote(buf.at[y, z], buf.at[y, z], send.at[i], recv.at[i], other, lon) for i, other in enumerate(z_tms)
        ]

    def both_y(buf, send, recv, i):
        k = (z + NZ - i) % NZ
        block = buf.at[y, k]
        return [
            remote(block, block, send.at[i, 0], recv.at[i, 0], y_next, lon),
            remote(block, block, send.at[i, 1], recv.at[i, 1], y_prev, lon),
        ]

    def relay_y(buf, send, recv, i, pair):
        k = (z + NZ - i) % NZ
        way = i % 2
        pair[way].wait_recv()
        block = buf.at[(y + NY - 1) % NY if way == 0 else (y + 1) % NY, k]
        copy = remote(block, block, send.at[i, 2], recv.at[i, 2], y_next if way == 0 else y_prev, lon)
        return [pair[way].wait_send, pair[1 - way].wait, copy.wait]

    az = all_z(gathered, az_s, az_r)
    order = (0, 1, 7, 2, 6, 3, 5, 4)
    ends = []
    previous = None
    for turn, i in enumerate(order):
        if i:
            az[i - 1].wait_recv()
            ends.append(az[i - 1].wait_send)
        pair = both_y(gathered, ay_s, ay_r, i)
        if previous is not None:
            ends += relay_y(gathered, ay_s, ay_r, *previous)
        previous = (i, pair)
        if turn == 5:
            from_low.wait()
            from_high.wait()
            low_rim = jnp.concatenate([lon_in[0] + 2.0 * value[:8] + value[8:16], value[:8] + 2.0 * value[8:16] + value[16:24]], axis=0)
            high_rim = jnp.concatenate([value[-24:-16] + 2.0 * value[-16:-8] + value[-8:], value[-16:-8] + 2.0 * value[-8:] + lon_in[1]], axis=0)
            rims[y, z] = jnp.stack([low_rim, high_rim]).astype(jnp.bfloat16)
            rz = all_z(rims, rz_s, rz_r)
    ends += relay_y(gathered, ay_s, ay_r, *previous)
    pairs = []
    for i in order:
        if i:
            rz[i - 1].wait_recv()
            ends.append(rz[i - 1].wait_send)
        pairs.append((i, both_y(rims, ry_s, ry_r, i)))

    matrix = elim[...]
    diagonal = jnp.sum(jnp.where(lane == row_of, matrix, 0.0), axis=1, keepdims=True)
    inverse = (matrix / jnp.sqrt(diagonal))[:, RANK:]
    basis = matmul(inverse, sketch, HI)
    series_out[...] = basis * math.sqrt(128 * days_blocks)
    basis_out[...] = contract_first(basis, inverse, HI).astype(jnp.bfloat16)

    for i, pair in pairs:
        ends += relay_y(rims, ry_s, ry_r, i, pair)
    for end in ends:
        end()

    def unpack_pair(source, at, pair):
        for c in range(NY):
            both = [source[c, k, at].astype(jnp.float32) for k in range(NZ)]
            cols = slice(128 * c, 128 * c + 128)
            for i in range(2):
                rows = jnp.concatenate([block[8 * i:8 * i + 8] for block in both], axis=0)
                patterns_out[2 * pair + i, :, cols] = rows.astype(jnp.bfloat16)

    def unpack(pair, carry):
        unpack_pair(gathered, pair - 1, pair)
        return carry

    lax.fori_loop(1, bands // 2 - 1, unpack, 0)
    unpack_pair(rims, 0, 0)
    unpack_pair(rims, 1, bands // 2 - 1)


def project(basis, patterns, out):
    for i in range(patterns.shape[0]):
        out[i] = matmul(basis[...], patterns[i]).astype(jnp.bfloat16)


def local(field, omega):
    days, bands, cols = field.shape
    pairs = bands // 2
    f32, bf16 = jnp.float32, jnp.bfloat16
    dma = pltpu.SemaphoreType.DMA
    vmem = pl.BlockSpec(memory_space=pltpu.VMEM)
    patterns, basis, series = pl.pallas_call(
        kernel,
        out_shape=(
            jax.ShapeDtypeStruct((bands, RANK, cols), bf16),
            jax.ShapeDtypeStruct((days, RANK), bf16),
            jax.ShapeDtypeStruct((RANK, days), f32),
        ),
        in_specs=[vmem] * 3,
        out_specs=(vmem,) * 3,
        scratch_shapes=[
            pltpu.VMEM((2, RANK, cols), bf16),
            pltpu.VMEM((bands + 2, RANK, cols), f32),
            pltpu.VMEM((NY - 1, bands, days, 128), bf16),
            pltpu.VMEM((NY, 2 * RANK, days), bf16),
            pltpu.VMEM((2, RANK, days), f32),
            pltpu.VMEM((NX, RANK, days), f32),
            pltpu.VMEM((2, RANK, days), f32),
            pltpu.VMEM((2, 16, days), f32),
            pltpu.VMEM((4, 16, days), f32),
            pltpu.VMEM((NZ, 32, 128), f32),
            pltpu.VMEM((NY, 32, 128), f32),
            pltpu.VMEM((NZ, pairs, 16, 128), bf16),
            pltpu.VMEM((NZ - 1, pairs, 16, 128), bf16),
            pltpu.VMEM((2, 8, 128), f32),
            pltpu.VMEM((2, 8, 128), f32),
            pltpu.VMEM((NY, NZ, pairs - 2, 16, 128), bf16),
            pltpu.VMEM((NY, NZ, 2, 16, 128), bf16),
            pltpu.VMEM((RANK, 128), f32),
            dma((2,)), dma((2,)), dma, dma, dma((3,)), dma((3,)), dma, dma, dma((4,)), dma((4,)),
            dma((7,)), dma((7,)), dma((3,)), dma((3,)), dma((3,)), dma((3,)), dma((3,)), dma((3,)), dma((7,)), dma((7,)),
            dma((2,)), dma((2,)), dma((7,)), dma((7,)), dma((8, 3)), dma((8, 3)),
            dma((7,)), dma((7,)), dma((8, 3)), dma((8, 3)),
        ],
        compiler_params=pltpu.CompilerParams(collective_id=0, has_side_effects=True),
        name="subspace",
    )(jnp.transpose(field, (1, 0, 2)), jnp.transpose(omega, (0, 2, 1)), jnp.asarray(toeplitz_blocks()))
    step = 6
    projected = pl.pallas_call(
        project,
        grid=(bands // step,),
        out_shape=jax.ShapeDtypeStruct((bands, days, cols), bf16),
        in_specs=[
            pl.BlockSpec((days, RANK), lambda i: (0, 0)),
            pl.BlockSpec((step, RANK, cols), lambda i: (i, 0, 0)),
        ],
        out_specs=pl.BlockSpec((step, days, cols), lambda i: (i, 0, 0)),
        name="project",
    )(basis, patterns)
    return jnp.transpose(projected, (1, 0, 2)), series.T


def solution(mesh):
    in_specs = (P("tm", "lon", None), P("lon", None, None))
    out_specs = (P("tm", "lon", None), P("tm", None))
    return jax.shard_map(local, mesh=mesh, in_specs=in_specs, out_specs=out_specs, check_vma=False)
```
